32 devices in a mesh: group: 4 (over x, core), dom: 8 (over z, y).
Axes of the slice: x: 2, y: 2, z: 4, core: 2. Of those that a mesh axis runs over, the one named last changes fastest.
Arguments:
- features: bfloat16 [16384, 512], P(('group', 'dom')), may hold values from -6 to 6
- w_query: bfloat16 [512, 512], replicated
- w_key: bfloat16 [512, 512], replicated
- w_value: bfloat16 [512, 512], replicated, may hold values from -0.25 to 0.25
- w_out: bfloat16 [512, 512], replicated, may hold values from -0.25 to 0.25
- w_up: bfloat16 [512, 2048], replicated, may hold values from -0.25 to 0.25
- w_down: bfloat16 [2048, 512], replicated, may hold values from -0.125 to 0.125
- block_len: int32 [128], P(('group', 'dom')), may hold values from 32 to 128, as said below
- cross_blocks: int32 [128, 2], P(('group', 'dom')), may hold values from 0 to 127, as said below
- cross_count: int32 [128], P(('group', 'dom')), may hold values from 1 to 2, as said below
Outputs:
- layer_out: bfloat16 [16384, 512], P(('group', 'dom'))
The draws below stay inside these ranges and needn't reach their ends.
Inputs may be any that keep to these rules, and one draw needn't show every extreme that they name: `block_len`: block 0 has all 128 nodes live. Block cross_blocks[b, c] lies in a group other than b's, at the same index of dom as block b, that is cross_blocks[b, c] // 4 % 8 == b // 4 % 8. `cross_count`: block 0 uses all 2 listed key blocks.
All inputs are finite; a program needn't handle non-finite values.
Results may differ from the reference program's by a relative error of at most 0.012.
The reference program's roundings to bfloat16 on the way count: a program that leaves them out, or rounds other values in their place, can miss the bound.
Values may be sent and summed in bfloat16 or wider, within the bound.
No kernel may reach another device: no remote copies, remote signals or barrier semaphores. Data moves between devices by JAX's collectives and lax.ppermute only.
A program may use at most 320 MiB of HBM per device.

```python
import jax
import jax.numpy as jnp
from jax import lax

D = 512
HEADS = 8
FF = 2048
BLK = 128
CROSS = 2
NB_DEV = 4
TOK_DEV = 512
NBLK = 128
NODES = 16384
N_GROUP = 4
N_DOM = 8


def projection_pair(key):
    base = jax.random.fold_in(key, 7)
    first = jax.random.normal(jax.random.fold_in(base, 1), (D, D), jnp.float32)
    second = jax.random.normal(jax.random.fold_in(base, 2), (D, D), jnp.float32)
    w_first = first * (3.0 / D ** 0.5)
    w_second = second * (1.0 / D ** 0.5)
    return (w_first, w_second)


def draw_w_query(key, part):
    return projection_pair(key)[0].astype(jnp.bfloat16)


def draw_w_key(key, part):
    return projection_pair(key)[1].astype(jnp.bfloat16)


def draw_block_len(key, part):
    lengths = jax.random.randint(jax.random.fold_in(key, 11), (NBLK,), BLK // 4, BLK + 1, jnp.int32)
    return lengths.at[0].set(BLK)


def draw_cross_blocks(key, part):
    block_ids = jnp.arange(NBLK, dtype=jnp.int32)
    group_ids = block_ids // (N_DOM * NB_DEV)
    dom_ids = block_ids // NB_DEV % N_DOM
    offsets = jax.random.randint(jax.random.fold_in(key, 21), (NBLK, CROSS), 1, N_GROUP, jnp.int32)
    locals_drawn = jax.random.randint(jax.random.fold_in(key, 22), (NBLK, CROSS), 0, NB_DEV, jnp.int32)
    other = (group_ids[:, None] + offsets) % N_GROUP
    return ((other * N_DOM + dom_ids[:, None]) * NB_DEV + locals_drawn).astype(jnp.int32)


def draw_cross_count(key, part):
    counts = jax.random.randint(jax.random.fold_in(key, 31), (NBLK,), 1, CROSS + 1, jnp.int32)
    return counts.at[0].set(CROSS)


def level_of(key, dims, pieces, smallest, high):
    factor_of, own = 1.0, jax.random.fold_in(key, 6)
    for position, parts in pieces:
        draws = jnp.exp(jax.random.uniform(jax.random.fold_in(own, position), (parts,), jnp.float32, smallest / len(pieces), high / len(pieces)))
        factor_of = factor_of * jnp.repeat(draws, dims[position] // parts).reshape([-1 if axis == position else 1 for axis in range(len(dims))])
    return factor_of


def normal_values(key, dims, width, reach, cuts=(), held_as=jnp.bfloat16):
    drawn = width * jax.random.normal(key, dims, jnp.float32)
    if cuts:
        drawn = drawn * level_of(key, dims, cuts, -0.22, 0.18)
    return jnp.clip(drawn, -reach, reach).astype(held_as)


def setup_inputs(seed: int = 0) -> dict:
    splits = jax.random.split(jax.random.key(seed), 11)
    features = normal_values(splits[0], (NODES, D), 1.0, 6.0, ((0, 32),))
    w_query = draw_w_query(jax.random.fold_in(splits[10], 71), 0)
    w_key = draw_w_key(jax.random.fold_in(splits[10], 71), 0)
    w_value = normal_values(splits[3], (D, D), D ** -0.5, 0.25)
    w_out = normal_values(splits[4], (D, D), D ** -0.5, 0.25)
    w_up = normal_values(splits[5], (D, FF), D ** -0.5, 0.25)
    w_down = normal_values(splits[6], (FF, D), FF ** -0.5, 0.125)
    block_len = draw_block_len(jax.random.fold_in(splits[10], 71), 0)
    cross_blocks = draw_cross_blocks(jax.random.fold_in(splits[10], 71), 0)
    cross_count = draw_cross_count(jax.random.fold_in(splits[10], 71), 0)
    return {"features": features, "w_query": w_query, "w_key": w_key, "w_value": w_value, "w_out": w_out, "w_up": w_up, "w_down": w_down, "block_len": block_len, "cross_blocks": cross_blocks, "cross_count": cross_count}


def rms_normed(values):
    wide = values.astype(jnp.float32)
    return (wide * lax.rsqrt(lax.optimization_barrier(jnp.mean(wide * wide, axis=-1, keepdims=True)) + 1e-06)).astype(jnp.bfloat16)

def attend(query_rows, key_rows, value_rows, live_mask):
    count_q = query_rows.shape[0]
    count_k = key_rows.shape[0]
    q_heads = query_rows.reshape(count_q, HEADS, -1).astype(jnp.float32)
    k_heads = key_rows.reshape(count_k, HEADS, -1).astype(jnp.float32)
    v_heads = value_rows.reshape(count_k, HEADS, -1).astype(jnp.float32)
    scale = 1.0 / q_heads.shape[-1] ** 0.5
    scores = jnp.einsum('rhd,shd->hrs', q_heads, k_heads) * scale
    scores = jnp.where(live_mask[None, None, :], scores, -1e+30)
    top = lax.optimization_barrier(jnp.max(scores, axis=-1, keepdims=True))
    weights = jnp.where(live_mask[None, None, :], jnp.exp(scores - top), 0.0)
    total = lax.optimization_barrier(jnp.sum(weights, axis=-1))
    rounded = lax.optimization_barrier(weights.astype(jnp.bfloat16)).astype(jnp.float32)
    summed = jnp.einsum('hrs,shd->rhd', rounded, v_heads)
    return (summed / jnp.transpose(total)[:, :, None]).reshape(count_q, -1)

def reference(features, w_query, w_key, w_value, w_out, w_up, w_down, block_len, cross_blocks, cross_count):
    nodes = features.shape[0]
    blocks = nodes // BLK
    live_blocks = jnp.arange(BLK, dtype=jnp.int32)[None, :] < block_len[:, None]
    live = live_blocks.reshape(nodes)
    normed = rms_normed(features)
    query = jnp.dot(normed, w_query, preferred_element_type=jnp.float32).astype(jnp.bfloat16)
    keys = jnp.dot(normed, w_key, preferred_element_type=jnp.float32).astype(jnp.bfloat16)
    values = jnp.dot(normed, w_value, preferred_element_type=jnp.float32).astype(jnp.bfloat16)
    group_nodes = TOK_DEV * N_DOM
    span_count = nodes // TOK_DEV

    def intra_span(index):
        start = (index * TOK_DEV).astype(jnp.int32)
        group_start = (index // N_DOM * group_nodes).astype(jnp.int32)
        q_rows = lax.dynamic_slice_in_dim(query, start, TOK_DEV, 0)
        k_rows = lax.dynamic_slice_in_dim(keys, group_start, group_nodes, 0)
        v_rows = lax.dynamic_slice_in_dim(values, group_start, group_nodes, 0)
        m_rows = lax.dynamic_slice_in_dim(live, group_start, group_nodes, 0)
        return attend(q_rows, k_rows, v_rows, m_rows)
    intra = lax.map(intra_span, jnp.arange(span_count, dtype=jnp.int32)).reshape(nodes, -1)
    key_blocks = keys.reshape(blocks, BLK, -1)
    value_blocks = values.reshape(blocks, BLK, -1)
    query_blocks = query.reshape(blocks, BLK, -1)

    def cross_block(index):
        chosen = cross_blocks[index]
        k_rows = key_blocks[chosen].reshape(CROSS * BLK, -1)
        v_rows = value_blocks[chosen].reshape(CROSS * BLK, -1)
        used = jnp.arange(CROSS, dtype=jnp.int32) < cross_count[index]
        m_rows = (live_blocks[chosen] & used[:, None]).reshape(CROSS * BLK)
        return attend(query_blocks[index], k_rows, v_rows, m_rows)
    cross = lax.map(cross_block, jnp.arange(blocks, dtype=jnp.int32)).reshape(nodes, -1)
    mixed = (intra + cross).astype(jnp.bfloat16)
    resid = (features.astype(jnp.float32) + jnp.dot(mixed, w_out, preferred_element_type=jnp.float32)).astype(jnp.bfloat16)
    normed_two = rms_normed(resid)
    hidden = jax.nn.gelu(jnp.dot(normed_two, w_up, preferred_element_type=jnp.float32)).astype(jnp.bfloat16)
    return (resid.astype(jnp.float32) + jnp.dot(hidden, w_down, preferred_element_type=jnp.float32)).astype(jnp.bfloat16)
```

```python
import jax
import jax.numpy as jnp
from jax import lax
from jax.experimental import pallas as pl
from jax.experimental.pallas import tpu as pltpu
from jax.sharding import PartitionSpec as P

HEADS = 8
CROSS = 2
BF = jnp.bfloat16
F32 = jnp.float32
DEAD = 1e30
DEAD_FROM = 1e29
LOG2E = 1.4426950408889634
ONES = 16
NT = (((1,), (1,)), ((), ()))


def vmem():
    return pl.BlockSpec(memory_space=pltpu.VMEM)


def smem():
    return pl.BlockSpec(memory_space=pltpu.SMEM)


def kernel_call(kernel, args, specs, outs, flops, name, aliases=None):
    moved = sum(a.size * a.dtype.itemsize for a in args) + sum(
        o.size * o.dtype.itemsize for o in outs
    )
    return pl.pallas_call(
        kernel,
        out_shape=tuple(outs),
        in_specs=specs,
        out_specs=tuple(vmem() for _ in outs),
        input_output_aliases=aliases or {},
        compiler_params=pltpu.CompilerParams(vmem_limit_bytes=40 << 20),
        cost_estimate=pl.CostEstimate(flops=flops, bytes_accessed=moved, transcendentals=0),
        name=name,
    )(*args)


def normed_rows(wide):
    return wide * lax.rsqrt(jnp.mean(wide * wide, axis=-1, keepdims=True) + 1e-06)


def norm_kernel(len_ref, feat_ref, out_ref):
    rows, width = feat_ref.shape
    blocks = len_ref.shape[0]
    per = rows // blocks
    place = lax.broadcasted_iota(jnp.int32, (per, width), 0)
    for b in range(blocks):
        span = slice(b * per, (b + 1) * per)
        row = normed_rows(feat_ref[span, :].astype(F32))
        out_ref[span, :] = jnp.where(place < len_ref[b], row, DEAD).astype(BF)


def keys_values(x, wk_ref, wvt_ref, spare):
    live = x[:, :1] < DEAD_FROM
    keys = jnp.dot(
        jnp.where(live, x, spare).astype(BF), wk_ref[...], preferred_element_type=F32
    ).astype(BF)
    vals = lax.dot_general(
        wvt_ref[...], jnp.where(live, x, 0.0).astype(BF), NT, preferred_element_type=F32
    ).astype(BF)
    flag = jnp.broadcast_to(jnp.where(live, 1.0, 0.0), (x.shape[0], 128)).astype(BF)
    lane = lax.broadcasted_iota(jnp.int32, (ONES, 128), 1)
    ones = lax.dot_general(
        jnp.where(lane == 0, 1.0, 0.0).astype(BF), flag, NT, preferred_element_type=F32
    ).astype(BF)
    return keys, vals, ones


def head_parts(keys, vals, ones, h):
    size = vals.shape[0] // HEADS
    pair = keys[:, h // 2 * 2 * size : (h // 2 + 1) * 2 * size]
    return (
        jnp.concatenate([pair, pair], axis=1),
        jnp.concatenate([vals[h * size : (h + 1) * size], ones], axis=0),
    )


def attend(x, qt_ref, wk_ref, wvt_ref, acc_ref, top_ref, first):
    keys, vals, ones = keys_values(x, wk_ref, wvt_ref, x[:1])
    for h in range(HEADS):
        pair, val = head_parts(keys, vals, ones, h)
        s = jnp.dot(pair, qt_ref[h], preferred_element_type=F32)
        top = jnp.max(s, axis=0, keepdims=True)
        if not first:
            before = top_ref[h : h + 1, :]
            top = jnp.maximum(before, top)
        p = jnp.exp2(s - top).astype(BF)
        added = jnp.dot(val, p, preferred_element_type=F32)
        if not first:
            added = acc_ref[h] * jnp.exp2(before - top) + added
        acc_ref[h] = added
        top_ref[h : h + 1, :] = top


def first_kernel(
    feat_ref, xs_ref, wq_ref, wk_ref, wv_ref, qt_ref, wvt_ref, acc_ref, top_ref
):
    rows = normed_rows(feat_ref[...].astype(F32)).astype(BF)
    wqt = jnp.transpose(wq_ref[...])
    wvt_ref[...] = jnp.transpose(wv_ref[...])
    size = wqt.shape[0] // HEADS
    query = lax.dot_general(wqt, rows, NT, preferred_element_type=F32).astype(BF).astype(F32)
    query = query * (LOG2E / size**0.5)
    high = query.astype(BF)
    low = (query - high.astype(F32)).astype(BF)
    none = jnp.zeros((size, rows.shape[0]), BF)
    for h in range(HEADS):
        span = slice(h * size, (h + 1) * size)
        parts = [high[span], none, low[span], none]
        if h % 2:
            parts = [none, high[span], none, low[span]]
        qt_ref[h] = jnp.concatenate(parts, axis=0)
    attend(xs_ref[...].astype(F32), qt_ref, wk_ref, wvt_ref, acc_ref, top_ref, True)


def more_kernel(count, *refs):
    parts = refs[:count]
    qt_ref, wk_ref, wvt_ref, acc_in, top_in, acc_ref, top_ref = refs[count:]
    acc_ref[...] = acc_in[...]
    top_ref[...] = top_in[...]
    for part in parts:
        attend(part[...].astype(F32), qt_ref, wk_ref, wvt_ref, acc_ref, top_ref, False)


def cross_kernel(slots, slot_ref, local_ref, count_ref, *refs):
    pieces = refs[:slots]
    qt_ref, wk_ref, wvt_ref, out_ref, sel_ref = refs[slots:]
    blocks = count_ref.shape[0]
    per = out_ref.shape[1] // blocks
    size = out_ref.shape[0] // HEADS
    for b in range(blocks):
        for c in range(CROSS):
            for s in range(slots):

                @pl.when(slot_ref[b * CROSS + c] == s)
                def _(b=b, c=c, s=s):
                    start = pl.multiple_of(local_ref[b * CROSS + c] * per, per)
                    sel_ref[pl.ds((b * CROSS + c) * per, per), :] = pieces[s][
                        pl.ds(start, per), :
                    ]

    for b in range(blocks):
        x = sel_ref[b * CROSS * per : (b + 1) * CROSS * per, :].astype(F32)
        place = lax.broadcasted_iota(jnp.int32, x.shape, 0)
        x = jnp.where(place < count_ref[b] * per, x, DEAD)
        keys, vals, ones = keys_values(x, wk_ref, wvt_ref, x[:1])
        for h in range(HEADS):
            pair, val = head_parts(keys, vals, ones, h)
            s = jnp.dot(pair, qt_ref[h, :, b * per : (b + 1) * per], preferred_element_type=F32)
            p = jnp.exp2(s - jnp.max(s, axis=0, keepdims=True)).astype(BF)
            added = jnp.dot(val, p, preferred_element_type=F32)
            out_ref[h * size : (h + 1) * size, b * per : (b + 1) * per] = (
                added[:size] / added[size : size + 1]
            )


def last_kernel(count, *refs):
    parts = refs[:count]
    (
        qt_ref,
        wk_ref,
        wvt_ref,
        acc_in,
        top_in,
        cross_ref,
        feat_ref,
        wo_ref,
        wu_ref,
        wd_ref,
        out_ref,
        acc_ref,
        top_ref,
    ) = refs[count:]
    acc_ref[...] = acc_in[...]
    top_ref[...] = top_in[...]
    for part in parts:
        attend(part[...].astype(F32), qt_ref, wk_ref, wvt_ref, acc_ref, top_ref, False)
    size = cross_ref.shape[0] // HEADS
    mixed = jnp.concatenate(
        [
            (
                acc_ref[h, :size] / acc_ref[h, size : size + 1]
                + cross_ref[h * size : (h + 1) * size, :]
            ).astype(BF)
            for h in range(HEADS)
        ],
        axis=0,
    )
    resid = (
        feat_ref[...].astype(F32)
        + jnp.dot(jnp.transpose(mixed), wo_ref[...], preferred_element_type=F32)
    ).astype(BF)
    wide = resid.astype(F32)
    rows = normed_rows(wide).astype(BF)
    step = 512
    total = wide
    for f in range(0, wu_ref.shape[1], step):
        hidden = jax.nn.gelu(
            jnp.dot(rows, wu_ref[:, f : f + step], preferred_element_type=F32)
        ).astype(BF)
        total = total + jnp.dot(hidden, wd_ref[f : f + step, :], preferred_element_type=F32)
    out_ref[...] = total.astype(BF)


def ring_order(mesh):
    count = mesh.shape["dom"]
    plain = list(range(count))
    line = mesh.devices[(0,) * (mesh.devices.ndim - 1)]
    at = [getattr(d, "coords", None) for d in line]
    if any(c is None for c in at):
        return plain
    axes = [i for i in range(3) if len({c[i] for c in at}) > 1]
    if len(axes) != 2:
        return plain
    sizes = [len({c[i] for c in at}) for i in axes]
    if sizes[0] * sizes[1] != count:
        return plain
    if sizes[0] % 2:
        axes, sizes = axes[::-1], sizes[::-1]
    if sizes[0] % 2:
        return plain
    low = [min(c[i] for c in at) for i in axes]
    where = {tuple(c[i] - lo for i, lo in zip(axes, low)): n for n, c in enumerate(at)}
    walk = []
    for row in range(sizes[0]):
        columns = list(range(1 if row else 0, sizes[1]))
        walk += [(row, col) for col in (columns[::-1] if row % 2 else columns)]
    walk += [(row, 0) for row in range(sizes[0] - 1, 0, -1)]
    if any(w not in where for w in walk):
        return plain
    return [where[w] for w in walk]


def make_body(order):
    count = len(order)
    forward = [(order[i], order[(i + 1) % count]) for i in range(count)]
    backward = [(b, a) for a, b in forward]

    def body(
        features, w_query, w_key, w_value, w_out, w_up, w_down, block_len, cross_blocks, cross_count
    ):
        rows, width = features.shape
        blocks = block_len.shape[0]
        groups = lax.axis_size("group")
        sds = jax.ShapeDtypeStruct
        size = width // HEADS
        (mine,) = kernel_call(
            norm_kernel, (block_len, features), [smem(), vmem()], [sds((rows, width), BF)],
            rows * width * 4, "norm",
        )

        ahead = behind = mine
        arrived = []
        for _ in range(count // 2 - 1):
            ahead = lax.ppermute(ahead, "dom", forward)
            behind = lax.ppermute(behind, "dom", backward)
            arrived.append((ahead, behind))
        half = rows // 2
        arrived.append(
            (
                lax.ppermute(ahead[:half], "dom", forward),
                lax.ppermute(behind[half:], "dom", backward),
            )
        )

        same = [mine] + [
            lax.ppermute(mine, "group", [(i, (i - 2 * k) % groups) for i in range(groups)])
            for k in range(1, groups // 2)
        ]
        swap = [(i, i ^ 1) for i in range(groups)]
        pieces = same + [lax.ppermute(s, "group", swap) for s in same]
        here = lax.axis_index("group")
        per_group = lax.axis_size("dom") * blocks
        chosen = cross_blocks.reshape(-1)
        group = chosen // per_group
        slot = (group // 2 - here // 2) % (groups // 2) + jnp.where(
            group % 2 == here % 2, 0, groups // 2
        )
        local = chosen % blocks

        state = (sds((HEADS, size + ONES, rows), F32), sds((HEADS, rows), F32))
        work = 2 * 4 * rows * rows * width * 2
        qt, wvt, acc, top = kernel_call(
            first_kernel,
            (features, mine, w_query, w_key, w_value),
            [vmem()] * 5,
            [sds((HEADS, 4 * size, rows), BF), sds((width, width), BF), *state],
            work,
            "first",
        )
        cross = None
        for turn, parts in enumerate(arrived[:-1]):
            acc, top = kernel_call(
                lambda *refs, n=len(parts): more_kernel(n, *refs),
                (*parts, qt, w_key, wvt, acc, top),
                [vmem()] * (len(parts) + 5),
                list(state),
                2 * work,
                f"more{turn}",
                {len(parts) + 3: 0, len(parts) + 4: 1},
            )
            if turn == 0:
                cross = pl.pallas_call(
                    lambda *refs, n=len(pieces): cross_kernel(n, *refs),
                    out_shape=sds((width, rows), F32),
                    in_specs=[smem()] * 3 + [vmem()] * (len(pieces) + 3),
                    out_specs=vmem(),
                    scratch_shapes=[pltpu.VMEM((rows * CROSS, width), BF)],
                    compiler_params=pltpu.CompilerParams(vmem_limit_bytes=40 << 20),
                    cost_estimate=pl.CostEstimate(
                        flops=work, bytes_accessed=8 << 20, transcendentals=0
                    ),
                    name="cross",
                )(slot, local, cross_count, *pieces, qt, w_key, wvt)
        parts = arrived[-1]
        return pl.pallas_call(
            lambda *refs, n=len(parts): last_kernel(n, *refs),
            out_shape=sds((rows, width), BF),
            in_specs=[vmem()] * (len(parts) + 10),
            out_specs=vmem(),
            scratch_shapes=[pltpu.VMEM(s.shape, F32) for s in state],
            compiler_params=pltpu.CompilerParams(vmem_limit_bytes=48 << 20),
            cost_estimate=pl.CostEstimate(
                flops=2 * work, bytes_accessed=16 << 20, transcendentals=0
            ),
            name="last",
        )(*parts, qt, w_key, wvt, acc, top, cross, features, w_out, w_up, w_down)

    return body


def solution(mesh):
    return jax.shard_map(
        make_body(ring_order(mesh)),
        mesh=mesh,
        in_specs=(
            P(("group", "dom"), None),
            P(),
            P(),
            P(),
            P(),
            P(),
            P(),
            P(("group", "dom")),
            P(("group", "dom"), None),
            P(("group", "dom")),
        ),
        out_specs=P(("group", "dom"), None),
        check_vma=False,
    )
```

```python
import jax
import jax.numpy as jnp
from jax import lax
from jax.experimental import pallas as pl
from jax.experimental.pallas import tpu as pltpu
from jax.sharding import PartitionSpec as P


HEADS = 8
CROSS = 2
BF = jnp.bfloat16
F32 = jnp.float32
DEAD = 1e30
DEAD_FROM = 1e29
LOG2E = 1.4426950408889634
ONES = 16
NT = (((1,), (1,)), ((), ()))


def vmem():
    return pl.BlockSpec(memory_space=pltpu.VMEM)


def smem():
    return pl.BlockSpec(memory_space=pltpu.SMEM)


def hbm():
    return pl.BlockSpec(memory_space=pltpu.HBM)


def kernel_call(kernel, args, specs, outs, flops, scratch=(), aliases=None, limit=24):
    moved = sum(a.size * a.dtype.itemsize for a in args) + sum(
        o.size * o.dtype.itemsize for o in outs
    )
    return pl.pallas_call(
        kernel,
        out_shape=tuple(outs),
        in_specs=specs,
        out_specs=tuple(vmem() for _ in outs),
        scratch_shapes=list(scratch),
        input_output_aliases=aliases or {},
        compiler_params=pltpu.CompilerParams(vmem_limit_bytes=limit << 20),
        cost_estimate=pl.CostEstimate(flops=flops, bytes_accessed=moved, transcendentals=0),
    )(*args)


def normed_rows(wide):
    return wide * lax.rsqrt(jnp.mean(wide * wide, axis=-1, keepdims=True) + 1e-06)


def start_copies(pairs, sems):
    copies = [pltpu.make_async_copy(a, b, sems.at[i]) for i, (a, b) in enumerate(pairs)]
    for copy in copies:
        copy.start()
    return copies


def norm_kernel(len_hbm, feat_hbm, out_ref, len_ref, feat_ref, sems):
    rows, width = feat_ref.shape
    blocks = len_ref.shape[0]
    per = rows // blocks
    spans = [slice(b * per, (b + 1) * per) for b in range(blocks)]
    copies = start_copies(
        [(len_hbm, len_ref)] + [(feat_hbm.at[s], feat_ref.at[s]) for s in spans], sems
    )
    copies[0].wait()
    place = lax.broadcasted_iota(jnp.int32, (per, width), 0)
    for b, span in enumerate(spans):
        copies[b + 1].wait()
        row = normed_rows(feat_ref[span, :].astype(F32))
        out_ref[span, :] = jnp.where(place < len_ref[b], row, DEAD).astype(BF)


def prepare(x, spare, span, xk_ref, xv_ref, flag_ref):
    live = x[:, :1] < DEAD_FROM
    xk_ref[span, :] = jnp.where(live, x, spare).astype(BF)
    xv_ref[span, :] = jnp.where(live, x, 0.0).astype(BF)
    flag_ref[span, :] = jnp.broadcast_to(
        jnp.where(live, 1.0, 0.0), (x.shape[0], flag_ref.shape[1])
    ).astype(BF)


def keys_values(xk_ref, xv_ref, flag_ref, wk_ref, wvt_ref):
    keys = jnp.dot(xk_ref[...], wk_ref[...], preferred_element_type=F32).astype(BF)
    vals = lax.dot_general(wvt_ref[...], xv_ref[...], NT, preferred_element_type=F32).astype(BF)
    lane = lax.broadcasted_iota(jnp.int32, (ONES, flag_ref.shape[1]), 1)
    ones = lax.dot_general(
        jnp.where(lane == 0, 1.0, 0.0).astype(BF), flag_ref[...], NT, preferred_element_type=F32
    ).astype(BF)
    return keys, vals, ones


def attend(xs, qt_ref, wk_ref, wvt_ref, acc_ref, top_ref, first):
    keys, vals, ones = keys_values(*xs, wk_ref, wvt_ref)
    size = vals.shape[0] // HEADS
    for h in range(HEADS):
        pair = keys[:, h // 2 * 2 * size : (h // 2 + 1) * 2 * size]
        s = jnp.dot(
            jnp.concatenate([pair, pair], axis=1), qt_ref[h], preferred_element_type=F32
        )
        top = jnp.max(s, axis=0, keepdims=True)
        if not first:
            before = top_ref[h : h + 1, :]
            top = jnp.maximum(before, top)
        p = jnp.exp2(s - top).astype(BF)
        val = jnp.concatenate([vals[h * size : (h + 1) * size], ones], axis=0)
        added = jnp.dot(val, p, preferred_element_type=F32)
        if not first:
            added = acc_ref[h] * jnp.exp2(before - top) + added
        acc_ref[h] = added
        top_ref[h : h + 1, :] = top


def first_kernel(
    xs_ref, feat_hbm, wq_hbm, wk_hbm, wv_hbm, qt_ref, wk_ref, wvt_ref, acc_ref, top_ref,
    feat_ref, wq_ref, wv_ref, sems, xk_ref, xv_ref, flag_ref,
):
    copies = start_copies(
        [(feat_hbm, feat_ref), (wq_hbm, wq_ref), (wv_hbm, wv_ref), (wk_hbm, wk_ref)], sems
    )
    x = xs_ref[...].astype(F32)
    prepare(x, x[:1], slice(None), xk_ref, xv_ref, flag_ref)
    copies[0].wait()
    rows = normed_rows(feat_ref[...].astype(F32)).astype(BF)
    copies[1].wait()
    wqt = jnp.transpose(wq_ref[...])
    size = wqt.shape[0] // HEADS
    query = lax.dot_general(wqt, rows, NT, preferred_element_type=F32).astype(BF).astype(F32)
    query = query * (LOG2E / size**0.5)
    high = query.astype(BF)
    low = (query - high.astype(F32)).astype(BF)
    none = jnp.zeros((size, rows.shape[0]), BF)
    for h in range(HEADS):
        span = slice(h * size, (h + 1) * size)
        parts = [high[span], none, low[span], none]
        if h % 2:
            parts = [none, high[span], none, low[span]]
        qt_ref[h] = jnp.concatenate(parts, axis=0)
    copies[2].wait()
    wvt_ref[...] = jnp.transpose(wv_ref[...])
    copies[3].wait()
    attend((xk_ref, xv_ref, flag_ref), qt_ref, wk_ref, wvt_ref, acc_ref, top_ref, True)


def each_part(parts, state_in, qt_ref, wk_ref, wvt_ref, state, xs):
    for here, there in zip(state_in, state):
        there[...] = here[...]

    def step(i, carry):
        for n, part in enumerate(parts):

            @pl.when(i == n)
            def _(part=part):
                x = part[...].astype(F32)
                prepare(x, x[:1], slice(None), *xs)

        attend(xs, qt_ref, wk_ref, wvt_ref, *state, False)
        return carry

    lax.fori_loop(0, len(parts), step, 0)


def more_kernel(count, *refs):
    qt_ref, wk_ref, wvt_ref, acc_in, top_in, acc_ref, top_ref, *xs = refs[count:]
    each_part(
        refs[:count], (acc_in, top_in), qt_ref, wk_ref, wvt_ref, (acc_ref, top_ref), xs
    )


def cross_kernel(slots, slot_ref, local_ref, count_ref, *refs):
    pieces = refs[:slots]
    qt_ref, wk_ref, wvt_ref, out_ref, sel_ref, k_ref, v_ref, o_ref, *xs = refs[slots:]
    blocks = count_ref.shape[0]
    per = out_ref.shape[1] // blocks
    span = CROSS * per
    size = out_ref.shape[0] // HEADS
    place = lax.broadcasted_iota(jnp.int32, (span, out_ref.shape[0]), 0)
    for b in range(blocks):
        for c in range(CROSS):
            n = b * CROSS + c
            for s in range(slots):

                @pl.when(slot_ref[n] == s)
                def _(n=n, s=s):
                    start = pl.multiple_of(local_ref[n] * per, per)
                    sel_ref[n * per : (n + 1) * per, :] = pieces[s][pl.ds(start, per), :]

        x = sel_ref[b * span : (b + 1) * span, :].astype(F32)
        x = jnp.where(place < count_ref[b] * per, x, DEAD)
        prepare(x, x[:1], slice(b * span, (b + 1) * span), *xs)
    keys, vals, ones = keys_values(*xs, wk_ref, wvt_ref)
    k_ref[...] = keys
    for b in range(blocks):
        v_ref[b] = vals[:, b * span : (b + 1) * span]
        o_ref[b] = ones[:, b * span : (b + 1) * span]

    for b in range(blocks):
        scores, probs = [], []
        for h in range(HEADS):
            pair = k_ref[b * span : (b + 1) * span, h // 2 * 2 * size : (h // 2 + 1) * 2 * size]
            s = jnp.dot(
                jnp.concatenate([pair, pair], axis=1),
                qt_ref[h, :, b * per : (b + 1) * per],
                preferred_element_type=F32,
            )
            scores.append(s)
        for s in scores:
            probs.append(jnp.exp2(s - jnp.max(s, axis=0, keepdims=True)).astype(BF))
        for h, p in enumerate(probs):
            val = jnp.concatenate([v_ref[b, h * size : (h + 1) * size], o_ref[b]], axis=0)
            added = jnp.dot(val, p, preferred_element_type=F32)
            out_ref[h * size : (h + 1) * size, b * per : (b + 1) * per] = (
                added[:size] / added[size : size + 1]
            )


def last_kernel(count, *refs):
    parts = refs[:count]
    (
        qt_ref, wk_ref, wvt_ref, acc_in, top_in, cross_ref, feat_hbm, wo_hbm, wu_hbm, wd_hbm,
        out_ref, acc_ref, top_ref, feat_ref, wo_ref, wu_ref, wd_ref, sems, *xs,
    ) = refs[count:]
    copies = start_copies(
        [(feat_hbm, feat_ref), (wo_hbm, wo_ref), (wu_hbm, wu_ref), (wd_hbm, wd_ref)], sems
    )
    half = parts[0].shape[0]
    for n, part in enumerate(parts):
        x = part[...].astype(F32)
        prepare(x, x[:1], slice(n * half, (n + 1) * half), *xs)
    acc_ref[...] = acc_in[...]
    top_ref[...] = top_in[...]
    attend(xs, qt_ref, wk_ref, wvt_ref, acc_ref, top_ref, False)
    size = cross_ref.shape[0] // HEADS
    mixed = jnp.concatenate(
        [
            (
                acc_ref[h, :size] / acc_ref[h, size : size + 1]
                + cross_ref[h * size : (h + 1) * size, :]
            ).astype(BF)
            for h in range(HEADS)
        ],
        axis=0,
    )
    copies[0].wait()
    copies[1].wait()
    resid = (
        feat_ref[...].astype(F32)
        + jnp.dot(jnp.transpose(mixed), wo_ref[...], preferred_element_type=F32)
    ).astype(BF)
    wide = resid.astype(F32)
    rows = normed_rows(wide).astype(BF)
    copies[2].wait()
    copies[3].wait()
    step = 512
    total = wide
    for f in range(0, wu_ref.shape[1], step):
        hidden = jax.nn.gelu(
            jnp.dot(rows, wu_ref[:, f : f + step], preferred_element_type=F32)
        ).astype(BF)
        total = total + jnp.dot(hidden, wd_ref[f : f + step, :], preferred_element_type=F32)
    out_ref[...] = total.astype(BF)


def ring_order(mesh):
    count = mesh.shape["dom"]
    plain = list(range(count))
    line = mesh.devices[(0,) * (mesh.devices.ndim - 1)]
    at = [getattr(d, "coords", None) for d in line]
    if any(c is None for c in at):
        return plain
    axes = [i for i in range(3) if len({c[i] for c in at}) > 1]
    if len(axes) != 2:
        return plain
    sizes = [len({c[i] for c in at}) for i in axes]
    if sizes[0] * sizes[1] != count:
        return plain
    if sizes[0] % 2:
        axes, sizes = axes[::-1], sizes[::-1]
    if sizes[0] % 2:
        return plain
    low = [min(c[i] for c in at) for i in axes]
    where = {tuple(c[i] - lo for i, lo in zip(axes, low)): n for n, c in enumerate(at)}
    walk = []
    for row in range(sizes[0]):
        columns = list(range(1 if row else 0, sizes[1]))
        walk += [(row, col) for col in (columns[::-1] if row % 2 else columns)]
    walk += [(row, 0) for row in range(sizes[0] - 1, 0, -1)]
    if any(w not in where for w in walk):
        return plain
    return [where[w] for w in walk]


def make_body(order):
    count = len(order)
    forward = [(order[i], order[(i + 1) % count]) for i in range(count)]
    backward = [(b, a) for a, b in forward]

    def body(
        features, w_query, w_key, w_value, w_out, w_up, w_down, block_len, cross_blocks, cross_count
    ):
        rows, width = features.shape
        blocks = block_len.shape[0]
        groups = lax.axis_size("group")
        sds = jax.ShapeDtypeStruct
        size = width // HEADS
        dma = pltpu.SemaphoreType.DMA

        def rows_scratch(n):
            return [pltpu.VMEM((n, width), BF), pltpu.VMEM((n, width), BF), pltpu.VMEM((n, 128), BF)]

        (mine,) = kernel_call(
            norm_kernel, (block_len, features), [hbm(), hbm()], [sds((rows, width), BF)],
            rows * width * 4,
            [pltpu.SMEM((blocks,), jnp.int32), pltpu.VMEM((rows, width), BF), dma((blocks + 1,))],
        )

        def hop(x, pairs):
            return lax.ppermute(x, "dom", pairs)

        ahead = behind = mine
        arrived = []
        for _ in range(count // 2 - 1):
            ahead = hop(ahead, forward)
            behind = hop(behind, backward)
            arrived.append((ahead, behind))
        half = rows // 2
        arrived.append((hop(ahead[:half], forward), hop(behind[half:], backward)))

        same = [mine] + [
            lax.ppermute(mine, "group", [(i, (i - 2 * k) % groups) for i in range(groups)])
            for k in range(1, groups // 2)
        ]
        swap = [(i, i ^ 1) for i in range(groups)]
        pieces = same + [lax.ppermute(s, "group", swap) for s in same]
        here = lax.axis_index("group")
        per_group = lax.axis_size("dom") * blocks
        chosen = cross_blocks.reshape(-1)
        group = chosen // per_group
        slot = (group // 2 - here // 2) % (groups // 2) + jnp.where(
            group % 2 == here % 2, 0, groups // 2
        )
        local = chosen % blocks

        state = [sds((HEADS, size + ONES, rows), F32), sds((HEADS, rows), F32)]
        work = 2 * 4 * rows * rows * width * 2
        square = sds((width, width), BF)
        qt, wk, wvt, acc, top = kernel_call(
            first_kernel,
            (mine, features, w_query, w_key, w_value),
            [vmem()] + [hbm()] * 4,
            [sds((HEADS, 4 * size, rows), BF), square, square, *state],
            work,
            [
                pltpu.VMEM((rows, width), BF),
                pltpu.VMEM((width, width), BF),
                pltpu.VMEM((width, width), BF),
                dma((4,)),
                *rows_scratch(rows),
            ],
        )
        cross = None
        for parts in arrived[:-1]:
            acc, top = kernel_call(
                lambda *refs, n=len(parts): more_kernel(n, *refs),
                (*parts, qt, wk, wvt, acc, top),
                [vmem()] * (len(parts) + 5),
                state,
                2 * work,
                rows_scratch(rows),
                {len(parts) + 3: 0, len(parts) + 4: 1},
            )
        picked = rows * CROSS
        span = picked // blocks
        (cross,) = kernel_call(
            lambda *refs, n=len(pieces): cross_kernel(n, *refs),
            (slot, local, cross_count, *pieces, qt, wk, wvt),
            [smem()] * 3 + [vmem()] * (len(pieces) + 3),
            [sds((width, rows), F32)],
            work,
            [
                pltpu.VMEM((picked, width), BF),
                pltpu.VMEM((picked, width), BF),
                pltpu.VMEM((blocks, width, span), BF),
                pltpu.VMEM((blocks, ONES, span), BF),
                *rows_scratch(picked),
            ],
        )
        parts = arrived[-1]
        (out,) = kernel_call(
            lambda *refs, n=len(parts): last_kernel(n, *refs),
            (*parts, qt, wk, wvt, acc, top, cross, features, w_out, w_up, w_down),
            [vmem()] * (len(parts) + 6) + [hbm()] * 4,
            [sds((rows, width), BF)],
            2 * work,
            [
                *(pltpu.VMEM(s.shape, F32) for s in state),
                pltpu.VMEM((rows, width), BF),
                *(pltpu.VMEM(w.shape, BF) for w in (w_out, w_up, w_down)),
                dma((4,)),
                *rows_scratch(rows),
            ],
        )
        return out

    return body


def solution(mesh):
    order = ring_order(mesh)
    inner = make_body(order)

    return jax.shard_map(
        inner,
        mesh=mesh,
        in_specs=(
            P(("group", "dom"), None),
            P(),
            P(),
            P(),
            P(),
            P(),
            P(),
            P(("group", "dom")),
            P(("group", "dom"), None),
            P(("group", "dom")),
        ),
        out_specs=P(("group", "dom"), None),
        check_vma=False,
    )
```

```python
import jax
import jax.numpy as jnp
from jax import lax
from jax.experimental import pallas as pl
from jax.experimental.pallas import tpu as pltpu
from jax.sharding import PartitionSpec as P


HEADS = 8
CROSS = 2
BF = jnp.bfloat16
F32 = jnp.float32
DEAD = 1e30
DEAD_FROM = 1e29
LOG2E = 1.4426950408889634
ONES = 16
NT = (((1,), (1,)), ((), ()))


def vmem():
    return pl.BlockSpec(memory_space=pltpu.VMEM)


def smem():
    return pl.BlockSpec(memory_space=pltpu.SMEM)


def hbm():
    return pl.BlockSpec(memory_space=pltpu.HBM)


def kernel_call(kernel, args, specs, outs, flops, scratch=(), aliases=None, limit=24):
    moved = sum(a.size * a.dtype.itemsize for a in args) + sum(
        o.size * o.dtype.itemsize for o in outs
    )
    return pl.pallas_call(
        kernel,
        out_shape=tuple(outs),
        in_specs=specs,
        out_specs=tuple(vmem() for _ in outs),
        scratch_shapes=list(scratch),
        input_output_aliases=aliases or {},
        compiler_params=pltpu.CompilerParams(vmem_limit_bytes=limit << 20),
        cost_estimate=pl.CostEstimate(flops=flops, bytes_accessed=moved, transcendentals=0),
    )(*args)


def normed_rows(wide):
    return wide * lax.rsqrt(jnp.mean(wide * wide, axis=-1, keepdims=True) + 1e-06)


def start_copies(pairs, sems):
    copies = [pltpu.make_async_copy(a, b, sems.at[i]) for i, (a, b) in enumerate(pairs)]
    for copy in copies:
        copy.start()
    return copies


def norm_kernel(len_hbm, feat_hbm, out_ref, len_ref, feat_ref, sems):
    rows, width = feat_ref.shape
    blocks = len_ref.shape[0]
    per = rows // blocks
    spans = [slice(b * per, (b + 1) * per) for b in range(blocks)]
    copies = start_copies(
        [(len_hbm, len_ref)] + [(feat_hbm.at[s], feat_ref.at[s]) for s in spans], sems
    )
    copies[0].wait()
    place = lax.broadcasted_iota(jnp.int32, (per, width), 0)
    for b, span in enumerate(spans):
        copies[b + 1].wait()
        row = normed_rows(feat_ref[span, :].astype(F32))
        out_ref[span, :] = jnp.where(place < len_ref[b], row, DEAD).astype(BF)


def load_part(x, spare, span, wk_ref, wvt_ref, k_ref, v_ref):
    live = x[:, :1] < jnp.asarray(DEAD_FROM, BF)
    rows = jnp.where(live, x, spare)
    flag = jnp.broadcast_to(jnp.where(live, jnp.ones((), BF), jnp.zeros((), BF)), (x.shape[0], 128))
    lane = lax.broadcasted_iota(jnp.int32, (ONES, 128), 1)
    ones = lax.dot_general(
        jnp.where(lane == 0, 1.0, 0.0).astype(BF), flag, NT, preferred_element_type=F32
    )
    keys = jnp.dot(rows, wk_ref[...], preferred_element_type=F32).astype(BF)
    vals = lax.dot_general(wvt_ref[...], rows, NT, preferred_element_type=F32)
    vals = (vals * ones[:1]).astype(BF)
    ones = ones.astype(BF)
    size = vals.shape[0] // HEADS
    for pair in range(HEADS // 2):
        k_ref[pair, span, :] = keys[:, pair * 2 * size : (pair + 1) * 2 * size]
    for h in range(HEADS):
        v_ref[h, :size, span] = vals[h * size : (h + 1) * size]
        v_ref[h, size:, span] = ones


def attend(qt_ref, k_ref, v_ref, even_ref, odd_ref, old, new):
    count = k_ref.shape[1]
    step = min(512, count)

    def scores(h, j, out_ref, top):
        pair = k_ref[h // 2 if isinstance(h, int) else lax.div(h, 2), j : j + step, :]
        s = jnp.dot(jnp.concatenate([pair, pair], axis=1), qt_ref[h], preferred_element_type=F32)
        out_ref[j : j + step, :] = s
        found = jnp.max(s, axis=0, keepdims=True)
        return found if top is None else jnp.maximum(top, found)

    def stage(h, in_ref, top, following, out_ref):
        total = None
        if old is not None:
            before = old[1][pl.ds(h, 1), :]
            top = jnp.maximum(before, top)
            total = old[0][h] * jnp.exp2(before - top)
        new[1][pl.ds(h, 1), :] = top
        found = None
        for j in range(0, count, step):
            if following is not None:
                found = scores(following, j, out_ref, found)
            p = jnp.exp2(in_ref[j : j + step, :] - top).astype(BF)
            added = jnp.dot(v_ref[h, :, j : j + step], p, preferred_element_type=F32)
            total = added if total is None else total + added
        new[0][h] = total
        return found

    def two(i, top):
        h = 2 * i
        top = stage(h, even_ref, top, h + 1, odd_ref)
        return stage(h + 1, odd_ref, top, h + 2, even_ref)

    top = None
    for j in range(0, count, step):
        top = scores(0, j, even_ref, top)
    top = lax.fori_loop(0, HEADS // 2 - 1, two, top)
    top = stage(HEADS - 2, even_ref, top, HEADS - 1, odd_ref)
    stage(HEADS - 1, odd_ref, top, None, None)


def first_kernel(
    xs_ref, feat_hbm, wq_hbm, wk_hbm, wv_hbm, qt_ref, wk_ref, wvt_ref, acc_ref, top_ref,
    feat_ref, wq_ref, wv_ref, sems, *work,
):
    copies = start_copies(
        [(feat_hbm, feat_ref), (wq_hbm, wq_ref), (wv_hbm, wv_ref), (wk_hbm, wk_ref)], sems
    )
    copies[0].wait()
    rows = normed_rows(feat_ref[...].astype(F32)).astype(BF)
    copies[1].wait()
    wqt = jnp.transpose(wq_ref[...])
    size = wqt.shape[0] // HEADS
    query = lax.dot_general(wqt, rows, NT, preferred_element_type=F32).astype(BF).astype(F32)
    query = query * (LOG2E / size**0.5)
    high = query.astype(BF)
    low = (query - high.astype(F32)).astype(BF)
    none = jnp.zeros((size, rows.shape[0]), BF)
    for h in range(HEADS):
        span = slice(h * size, (h + 1) * size)
        parts = [high[span], none, low[span], none]
        if h % 2:
            parts = [none, high[span], none, low[span]]
        qt_ref[h] = jnp.concatenate(parts, axis=0)
    copies[2].wait()
    wvt_ref[...] = jnp.transpose(wv_ref[...])
    copies[3].wait()
    x = xs_ref[...]
    load_part(x, x[:1], slice(None), wk_ref, wvt_ref, *work[:2])
    attend(qt_ref, *work, None, (acc_ref, top_ref))


def all_parts(parts, wk_ref, wvt_ref, k_ref, v_ref):
    start = 0
    for part in parts:
        x = part[...]
        load_part(x, x[:1], slice(start, start + x.shape[0]), wk_ref, wvt_ref, k_ref, v_ref)
        start += x.shape[0]


def more_kernel(count, *refs):
    qt_ref, wk_ref, wvt_ref, acc_in, top_in, acc_ref, top_ref, *work = refs[count:]
    all_parts(refs[:count], wk_ref, wvt_ref, *work[:2])
    attend(qt_ref, *work, (acc_in, top_in), (acc_ref, top_ref))


def cross_kernel(slots, slot_ref, local_ref, count_ref, *refs):
    pieces = refs[:slots]
    qt_ref, wk_ref, wvt_ref, out_ref, sel_ref, k_ref, v_ref = refs[slots:]
    blocks = count_ref.shape[0]
    per = out_ref.shape[1] // blocks
    span = CROSS * per
    size = out_ref.shape[0] // HEADS
    place = lax.broadcasted_iota(jnp.int32, (span, 1), 0)
    for b in range(blocks):
        for c in range(CROSS):
            n = b * CROSS + c
            for s in range(slots):

                @pl.when(slot_ref[n] == s)
                def _(n=n, s=s):
                    start = pl.multiple_of(local_ref[n] * per, per)
                    sel_ref[n * per : (n + 1) * per, :] = pieces[s][pl.ds(start, per), :]

        used = jnp.where(place < count_ref[b] * per, 0.0, DEAD).astype(BF)
        x = sel_ref[b * span : (b + 1) * span, :]
        load_part(
            jnp.where(used > 0, used, x),
            x[:1], slice(b * span, (b + 1) * span), wk_ref, wvt_ref, k_ref, v_ref,
        )

    def scores(h, b):
        pair = k_ref[h // 2, b * span : (b + 1) * span, :]
        return jnp.dot(
            jnp.concatenate([pair, pair], axis=1),
            qt_ref[h, :, b * per : (b + 1) * per],
            preferred_element_type=F32,
        )

    turns = [(h, b) for h in range(HEADS) for b in range(blocks)]
    lag = 4
    held = []
    for n in range(len(turns) + lag):
        if n < len(turns):
            held.append(scores(*turns[n]))
        if n >= lag:
            h, b = turns[n - lag]
            s = held[n - lag]
            p = jnp.exp2(s - jnp.max(s, axis=0, keepdims=True)).astype(BF)
            added = jnp.dot(
                v_ref[h, :, b * span : (b + 1) * span], p, preferred_element_type=F32
            )
            out_ref[h * size : (h + 1) * size, b * per : (b + 1) * per] = (
                added[:size] / added[size : size + 1]
            )


def last_kernel(count, *refs):
    (
        qt_ref, wk_ref, wvt_ref, acc_in, top_in, cross_ref, feat_ref, wo_ref, wu_ref, wd_ref,
        out_ref, acc_ref, top_ref, *work,
    ) = refs[count:]
    all_parts(refs[:count], wk_ref, wvt_ref, *work[:2])
    attend(qt_ref, *work, (acc_in, top_in), (acc_ref, top_ref))
    size = cross_ref.shape[0] // HEADS
    mixed = jnp.concatenate(
        [
            (
                acc_ref[h, :size] / acc_ref[h, size : size + 1]
                + cross_ref[h * size : (h + 1) * size, :]
            ).astype(BF)
            for h in range(HEADS)
        ],
        axis=0,
    )
    resid = (
        feat_ref[...].astype(F32)
        + jnp.dot(jnp.transpose(mixed), wo_ref[...], preferred_element_type=F32)
    ).astype(BF)
    wide = resid.astype(F32)
    rows = normed_rows(wide).astype(BF)
    step = 512
    total = wide
    for f in range(0, wu_ref.shape[1], step):
        hidden = jax.nn.gelu(
            jnp.dot(rows, wu_ref[:, f : f + step], preferred_element_type=F32)
        ).astype(BF)
        total = total + jnp.dot(hidden, wd_ref[f : f + step, :], preferred_element_type=F32)
    out_ref[...] = total.astype(BF)


def ring_order(mesh):
    count = mesh.shape["dom"]
    plain = list(range(count))
    line = mesh.devices[(0,) * (mesh.devices.ndim - 1)]
    at = [getattr(d, "coords", None) for d in line]
    if any(c is None for c in at):
        return plain
    axes = [i for i in range(3) if len({c[i] for c in at}) > 1]
    if len(axes) != 2:
        return plain
    sizes = [len({c[i] for c in at}) for i in axes]
    if sizes[0] * sizes[1] != count:
        return plain
    if sizes[0] % 2:
        axes, sizes = axes[::-1], sizes[::-1]
    if sizes[0] % 2:
        return plain
    low = [min(c[i] for c in at) for i in axes]
    where = {tuple(c[i] - lo for i, lo in zip(axes, low)): n for n, c in enumerate(at)}
    walk = []
    for row in range(sizes[0]):
        columns = list(range(1 if row else 0, sizes[1]))
        walk += [(row, col) for col in (columns[::-1] if row % 2 else columns)]
    walk += [(row, 0) for row in range(sizes[0] - 1, 0, -1)]
    if any(w not in where for w in walk):
        return plain
    return [where[w] for w in walk]


def make_body(order):
    count = len(order)
    forward = [(order[i], order[(i + 1) % count]) for i in range(count)]
    backward = [(b, a) for a, b in forward]

    def body(
        features, w_query, w_key, w_value, w_out, w_up, w_down, block_len, cross_blocks, cross_count
    ):
        rows, width = features.shape
        blocks = block_len.shape[0]
        groups = lax.axis_size("group")
        sds = jax.ShapeDtypeStruct
        size = width // HEADS
        dma = pltpu.SemaphoreType.DMA

        def key_scratch(n):
            return [
                pltpu.VMEM((HEADS // 2, n, 2 * size), BF),
                pltpu.VMEM((HEADS, size + ONES, n), BF),
            ]

        def work_scratch(n):
            return key_scratch(n) + [pltpu.VMEM((n, rows), F32)] * 2

        (mine,) = kernel_call(
            norm_kernel, (block_len, features), [hbm(), hbm()], [sds((rows, width), BF)],
            rows * width * 4,
            [pltpu.SMEM((blocks,), jnp.int32), pltpu.VMEM((rows, width), BF), dma((blocks + 1,))],
        )

        def hop(x, pairs):
            return lax.ppermute(x, "dom", pairs)

        ahead = behind = mine
        arrived = []
        for _ in range(count // 2 - 1):
            ahead = hop(ahead, forward)
            behind = hop(behind, backward)
            arrived.append((ahead, behind))
        half = rows // 2
        arrived.append((hop(ahead[:half], forward), hop(behind[half:], backward)))

        same = [mine] + [
            lax.ppermute(mine, "group", [(i, (i - 2 * k) % groups) for i in range(groups)])
            for k in range(1, groups // 2)
        ]
        swap = [(i, i ^ 1) for i in range(groups)]
        pieces = same + [lax.ppermute(s, "group", swap) for s in same]
        here = lax.axis_index("group")
        per_group = lax.axis_size("dom") * blocks
        chosen = cross_blocks.reshape(-1)
        group = chosen // per_group
        slot = (group // 2 - here // 2) % (groups // 2) + jnp.where(
            group % 2 == here % 2, 0, groups // 2
        )
        local = chosen % blocks

        state = [sds((HEADS, size + ONES, rows), F32), sds((HEADS, rows), F32)]
        work = 2 * 4 * rows * rows * width * 2
        square = sds((width, width), BF)
        qt, wk, wvt, acc, top = kernel_call(
            first_kernel,
            (mine, features, w_query, w_key, w_value),
            [vmem()] + [hbm()] * 4,
            [sds((HEADS, 4 * size, rows), BF), square, square, *state],
            work,
            [
                pltpu.VMEM((rows, width), BF),
                pltpu.VMEM((width, width), BF),
                pltpu.VMEM((width, width), BF),
                dma((4,)),
                *work_scratch(rows),
            ],
        )
        for parts in arrived[:-1]:
            acc, top = kernel_call(
                lambda *refs, n=len(parts): more_kernel(n, *refs),
                (*parts, qt, wk, wvt, acc, top),
                [vmem()] * (len(parts) + 5),
                state,
                2 * work,
                work_scratch(len(parts) * rows),
                {len(parts) + 3: 0, len(parts) + 4: 1},
            )
        picked = rows * CROSS
        (cross,) = kernel_call(
            lambda *refs, n=len(pieces): cross_kernel(n, *refs),
            (slot, local, cross_count, *pieces, qt, wk, wvt),
            [smem()] * 3 + [vmem()] * (len(pieces) + 3),
            [sds((width, rows), F32)],
            work,
            [
                pltpu.VMEM((picked, width), BF),
                *key_scratch(picked),
            ],
        )
        parts = arrived[-1]
        (out,) = kernel_call(
            lambda *refs, n=len(parts): last_kernel(n, *refs),
            (*parts, qt, wk, wvt, acc, top, cross, features, w_out, w_up, w_down),
            [vmem()] * (len(parts) + 10),
            [sds((rows, width), BF)],
            2 * work,
            [
                *(pltpu.VMEM(s.shape, F32) for s in state),
                *work_scratch(2 * half),
            ],
        )
        return out

    return body


def solution(mesh):
    order = ring_order(mesh)
    inner = make_body(order)

    return jax.shard_map(
        inner,
        mesh=mesh,
        in_specs=(
            P(("group", "dom"), None),
            P(),
            P(),
            P(),
            P(),
            P(),
            P(),
            P(("group", "dom")),
            P(("group", "dom"), None),
            P(("group", "dom")),
        ),
        out_specs=P(("group", "dom"), None),
        check_vma=False,
    )
```
